32 devices in a mesh: groups: 2 (over x), req: 16 (over z, y, core).
Axes of the slice: x: 2, y: 2, z: 4, core: 2. Of those that a mesh axis runs over, the one named last changes fastest.
Arguments:
- queries: bfloat16 [64, 128, 192], P('groups', 'req'), parts along dimension 0, may hold values from -48 to 48
- absorb_key: bfloat16 [128, 128, 512], P('req'), may hold values from -0.5 to 0.5
- absorb_value: bfloat16 [128, 512, 128], P('req'), may hold values from -0.75 to 0.75
- out_weight: bfloat16 [16384, 5120], P('req'), may hold values from -0.046875 to 0.046875
- latent_cache: bfloat16 [64, 4096, 576], P(('groups', 'req')), parts along dimension 0, may hold values from -12 to 12
- lengths: int32 [64], P(('groups', 'req')), parts along dimension 0, may hold values from 2 to 4096, as said below
- slot_request: int32 [64], P('groups'), parts along dimension 0, may hold values from 0 to 31, each once
Outputs:
- attended: bfloat16 [64, 5120], P(('groups', 'req')), parts along dimension 0
The draws below stay inside these ranges and needn't reach their ends.
There are 2 independent parts, one for each index of `groups`. The reference program is written for one: setup_inputs(seed, part) draws one part's arguments, and reference() takes and returns one part's arrays. A program takes and returns all parts, laid end to end along the dimension named above; an argument that names none is the same for every part. Nothing has to cross between parts.
Inputs may be any that keep to these rules, and one draw needn't show every extreme that they name: Slot j's valid positions are its first lengths[j] ones; some slot of each group holds exactly 4096. `slot_request`: each request stands in exactly one slot.
All inputs are finite; a program needn't handle non-finite values.
Results may differ from the reference program's by a relative error of at most 0.0079.
Values may be sent and summed in bfloat16 or wider, within the bound.
A program may use at most 64 MiB of HBM per device.

```python
import math
import jax
import jax.numpy as jnp
from jax import lax

D = 5120
HEADS = 128
NOPE = 128
ROPE = 64
LATENT = 512
VDIM = 128
CTX = 4096
REQS = 32


def draw_queries(key, part):
    shape = (REQS, HEADS, NOPE + ROPE)
    return jnp.clip(1.5 * jax.random.normal(jax.random.fold_in(key, 2), shape, jnp.float32), -9.0, 9.0).astype(jnp.bfloat16)


def draw_latent_cache(key, part):
    shape = (REQS, CTX, LATENT + ROPE)
    return jnp.clip(jax.random.normal(jax.random.fold_in(key, 4), shape, jnp.float32), -6.0, 6.0).astype(jnp.bfloat16)


def draw_lengths(key, part):
    drawn = jax.random.randint(jax.random.fold_in(key, 5), (REQS,), 2, CTX + 1)
    longest = jax.random.randint(jax.random.fold_in(key, 6), (), 0, REQS)
    slots = jnp.arange(REQS)
    return jnp.where(slots == longest, CTX, drawn).astype(jnp.int32)


def levels(rng, shape, shards, smallest, top_value):
    level = 1.0
    for axis_at, parts in shards:
        draws = jax.random.uniform(jax.random.fold_in(jax.random.fold_in(rng, 6), axis_at), (parts,), jnp.float32, smallest / len(shards), top_value / len(shards))
        level = level * jnp.repeat(jnp.exp(draws), shape[axis_at] // parts).reshape((-1,) + (1,) * (len(shape) - 1 - axis_at))
    return level


def noise(stream_key, extent, scale, limit, pieces=(), held_as=jnp.bfloat16):
    result = scale * jax.random.normal(stream_key, extent, jnp.float32)
    if pieces:
        result = result * levels(stream_key, extent, pieces, -0.22, 0.18)
    return jnp.clip(result, -limit, limit).astype(held_as)


def setup_inputs(seed: int = 0, part: int = 0) -> dict:
    keys = jax.random.split(jax.random.key(seed), 8)
    part_keys = jax.random.split(jax.random.fold_in(keys[7], part), 8)
    queries = draw_queries(jax.random.fold_in(jax.random.fold_in(keys[7], part), 71), part)
    absorb_key = noise(keys[1], (HEADS, NOPE, LATENT), NOPE ** -0.5, 0.5, ((0, 16),))
    absorb_value = noise(keys[2], (HEADS, LATENT, VDIM), (LATENT // 8) ** -0.5, 0.75, ((0, 16),))
    out_weight = noise(keys[3], (HEADS * VDIM, D), (HEADS * VDIM) ** -0.5, 0.046875, ((0, 16),))
    latent_cache = draw_latent_cache(jax.random.fold_in(jax.random.fold_in(keys[7], part), 71), part)
    lengths = draw_lengths(jax.random.fold_in(jax.random.fold_in(keys[7], part), 71), part)
    slot_request = jax.random.permutation(part_keys[6], REQS).astype(jnp.int32)
    return dict(queries=queries, absorb_key=absorb_key, absorb_value=absorb_value, out_weight=out_weight, latent_cache=latent_cache, lengths=lengths, slot_request=slot_request)


def attend_slot(absorbed_row, cache_row, length):
    factor = 1.0 / math.sqrt(NOPE + ROPE)
    scores = jnp.dot(absorbed_row, cache_row.T, preferred_element_type=jnp.float32) * factor
    visible = jnp.arange(CTX) < length
    scores = jnp.where(visible[None, :], scores, -jnp.inf)
    highest = lax.optimization_barrier(jnp.max(scores, axis=1, keepdims=True))
    weights = jnp.exp(scores - highest)
    probs = (weights / lax.optimization_barrier(jnp.sum(weights, axis=1, keepdims=True))).astype(jnp.bfloat16)
    return jnp.dot(probs, cache_row[:, :LATENT], preferred_element_type=jnp.float32).astype(jnp.bfloat16)

def reference(queries, absorb_key, absorb_value, out_weight, latent_cache, lengths, slot_request):
    ordered = jnp.take(queries, slot_request, axis=0)
    lifted = jnp.einsum('jhn,hnc->jhc', ordered[:, :, :NOPE].astype(jnp.float32), absorb_key.astype(jnp.float32))
    absorbed = jnp.concatenate([lifted, ordered[:, :, NOPE:].astype(jnp.float32)], axis=2).astype(jnp.bfloat16)
    latent = lax.map(lambda item: attend_slot(item[0], item[1], item[2]), (absorbed, latent_cache, lengths))
    values = jnp.einsum('jhc,hcv->jhv', latent.astype(jnp.float32), absorb_value.astype(jnp.float32)).astype(jnp.bfloat16)
    flattened = values.reshape(REQS, HEADS * VDIM)
    return jnp.dot(flattened, out_weight, preferred_element_type=jnp.float32).astype(jnp.bfloat16)
```

```python
import functools
import math

import jax
import jax.numpy as jnp
from jax import lax
from jax.experimental import pallas as pl
from jax.experimental.pallas import tpu as pltpu
from jax.sharding import PartitionSpec as P

MESH = pl.DeviceIdType.MESH
LANES = 128
SCORE_TILE = 1024
OUT_TILES = 5


def kernel(
    n, request_ref, length_ref, query_ref, key_hbm, value_hbm, weight_hbm, cache_hbm,
    out_ref,
    key, value, weight, cache, query_rows, rotary_rows, absorbed_rows, absorbed_out, absorbed_in,
    slot_rows, scores, latent_rows, latent_out, latent_in, returned_rows, values,
    partial, partial_out, partial_in,
    load_sem, send_a, recv_a, send_b, recv_b, send_c, recv_c,
):
    requests, heads, width = query_ref.shape
    nope, latent = key_hbm.shape[1:]
    vdim = value_hbm.shape[2]
    slots, _, context = cache_hbm.shape
    tiles = partial_out.shape[0]
    tile = partial_out.shape[3]
    lanes = latent // LANES
    me = lax.axis_index("req")

    barrier = pltpu.get_barrier_semaphore()

    def greet(k, carry):
        pl.semaphore_signal(
            barrier, inc=1, device_id={"req": lax.rem(me + k, n)}, device_id_type=MESH
        )
        return carry

    lax.fori_loop(1, n, greet, 0)

    load_key = pltpu.make_async_copy(key_hbm, key, load_sem.at[0])
    load_value = pltpu.make_async_copy(value_hbm, value, load_sem.at[1])
    load_weight = pltpu.make_async_copy(weight_hbm, weight, load_sem.at[2])
    load_cache = [
        pltpu.make_async_copy(cache_hbm.at[s], cache.at[s], load_sem.at[3 + s])
        for s in range(slots)
    ]
    load_key.start()
    load_cache[0].start()

    for j in range(requests):
        row = query_ref[request_ref[j]].astype(jnp.float32)
        query_rows[j * heads : (j + 1) * heads, :] = row[:, :nope]
        rotary_rows[j * heads : (j + 1) * heads, :] = row[:, nope:]
    load_key.wait()
    for s in range(1, slots):
        load_cache[s].start()
    load_value.start()
    load_weight.start()
    for h in range(heads):
        picked = query_rows[pl.ds(h, requests, stride=heads), :].astype(jnp.bfloat16)
        lifted = jnp.dot(picked, key[h], preferred_element_type=jnp.float32)
        for l in range(lanes):
            absorbed_rows[l, pl.ds(h, requests, stride=heads), :] = lifted[
                :, l * LANES : (l + 1) * LANES
            ]

    def exchange(out, into, send_sem, recv_sem, at):
        def copy(to, source):
            return pltpu.make_async_remote_copy(
                src_ref=out.at[at, to],
                dst_ref=into.at[at, source],
                send_sem=send_sem.at[at, to],
                recv_sem=recv_sem.at[at, source],
                device_id={"req": to},
                device_id_type=MESH,
            )

        def start(k, carry):
            copy(lax.rem(me + k, n), me).start()
            return carry

        def arrive(k, carry):
            other = lax.rem(me + n - k, n)
            copy(other, other).wait_recv()
            return carry

        def leave(k, carry):
            copy(lax.rem(me + k, n), me).wait_send()
            return carry

        return (
            lambda: lax.fori_loop(1, n, start, 0),
            lambda: lax.fori_loop(1, n, arrive, 0),
            lambda: lax.fori_loop(1, n, leave, 0),
        )

    queries_of = [exchange(absorbed_out, absorbed_in, send_a, recv_a, s) for s in range(slots)]
    latents_of = [exchange(latent_out, latent_in, send_b, recv_b, s) for s in range(slots)]
    partials_of = [exchange(partial_out, partial_in, send_c, recv_c, c) for c in range(tiles)]

    for s in range(slots):
        for d in range(n):
            row = (d * slots + s) * heads
            for l in range(lanes):
                absorbed_out[s, d, :, l * LANES : (l + 1) * LANES] = absorbed_rows[
                    l, row : row + heads, :
                ].astype(jnp.bfloat16)
            absorbed_out[s, d, :, latent:] = rotary_rows[row : row + heads, :].astype(jnp.bfloat16)
        if s == 0:
            pl.semaphore_wait(barrier, n - 1)
        queries_of[s][0]()
        absorbed_in[s, me] = absorbed_out[s, me]

    scale = math.log2(math.e) / math.sqrt(width)
    for s in range(slots):
        queries_of[s][1]()
        for i in range(n):
            slot_rows[i * heads : (i + 1) * heads, :] = absorbed_in[s, i].astype(jnp.float32)
        query = slot_rows[...].astype(jnp.bfloat16)
        load_cache[s].wait()
        length = length_ref[s]
        highest = None
        for t in range(0, context, SCORE_TILE):
            score = jnp.dot(
                query, cache[s, :, t : t + SCORE_TILE], preferred_element_type=jnp.float32
            )
            position = t + lax.broadcasted_iota(jnp.int32, (1, SCORE_TILE), 1)
            score = jnp.where(position < length, score, -jnp.inf)
            scores[:, t : t + SCORE_TILE] = score
            top = jnp.max(score, axis=1, keepdims=True)
            highest = top if highest is None else jnp.maximum(highest, top)
        total, mixed = None, None
        for t in range(0, context, SCORE_TILE):
            prob = jnp.exp2((scores[:, t : t + SCORE_TILE] - highest) * scale)
            part = jnp.sum(prob, axis=1, keepdims=True)
            product = lax.dot_general(
                prob.astype(jnp.bfloat16),
                cache[s, :latent, t : t + SCORE_TILE],
                (((1,), (1,)), ((), ())),
                preferred_element_type=jnp.float32,
            )
            total = part if total is None else total + part
            mixed = product if mixed is None else mixed + product
        latent_rows[...] = mixed / total
        for i in range(n):
            latent_out[s, i] = latent_rows[i * heads : (i + 1) * heads, :].astype(jnp.bfloat16)
        latents_of[s][0]()
        latent_in[s, me] = latent_out[s, me]

    load_value.wait()
    for s in range(slots):
        latents_of[s][1]()
        for d in range(n):
            row = (d * slots + s) * heads
            for l in range(lanes):
                returned_rows[l, row : row + heads, :] = latent_in[
                    s, d, :, l * LANES : (l + 1) * LANES
                ].astype(jnp.float32)
    for h in range(heads):
        picked = jnp.concatenate(
            [returned_rows[l, pl.ds(h, requests, stride=heads), :] for l in range(lanes)], axis=1
        ).astype(jnp.bfloat16)
        values[:, h * vdim : (h + 1) * vdim] = jnp.dot(
            picked, value[h], preferred_element_type=jnp.float32
        ).astype(jnp.bfloat16)

    load_weight.wait()
    for c in range(tiles):
        partial[...] = jnp.dot(
            values[...], weight[:, c * tile : (c + 1) * tile], preferred_element_type=jnp.float32
        )
        for d in range(n):
            partial_out[c, d] = partial[d * slots : (d + 1) * slots, :].astype(jnp.bfloat16)
        partials_of[c][0]()
        partial_in[c, me] = partial_out[c, me]
    for c in range(tiles):
        partials_of[c][1]()
        summed = partial_in[c, 0].astype(jnp.float32)
        for i in range(1, n):
            summed = summed + partial_in[c, i].astype(jnp.float32)
        out_ref[:, c * tile : (c + 1) * tile] = summed.astype(jnp.bfloat16)

    for pending in queries_of + latents_of + partials_of:
        pending[2]()


def on_device(n, queries, absorb_key, absorb_value, out_weight, latent_cache, lengths, slot_request):
    cache = jnp.swapaxes(latent_cache, 1, 2)
    requests, heads, width = queries.shape
    slots, key_width, context = cache.shape
    nope, latent = absorb_key.shape[1:]
    model = out_weight.shape[1]
    rows = requests * heads
    tile = model // OUT_TILES
    vmem, smem, anywhere = (
        pl.BlockSpec(memory_space=space) for space in (pltpu.VMEM, pltpu.SMEM, pl.ANY)
    )
    low, wide = jnp.bfloat16, jnp.float32
    return pl.pallas_call(
        functools.partial(kernel, n),
        out_shape=jax.ShapeDtypeStruct((slots, model), low),
        in_specs=[smem, smem, vmem, anywhere, anywhere, anywhere, anywhere],
        out_specs=vmem,
        scratch_shapes=[
            pltpu.VMEM(absorb_key.shape, low),
            pltpu.VMEM(absorb_value.shape, low),
            pltpu.VMEM(out_weight.shape, low),
            pltpu.VMEM(cache.shape, low),
            pltpu.VMEM((rows, nope), wide),
            pltpu.VMEM((rows, width - nope), wide),
            pltpu.VMEM((latent // LANES, rows, LANES), wide),
            pltpu.VMEM((slots, n, heads, key_width), low),
            pltpu.VMEM((slots, n, heads, key_width), low),
            pltpu.VMEM((n * heads, key_width), wide),
            pltpu.VMEM((n * heads, context), wide),
            pltpu.VMEM((n * heads, latent), wide),
            pltpu.VMEM((slots, n, heads, latent), low),
            pltpu.VMEM((slots, n, heads, latent), low),
            pltpu.VMEM((latent // LANES, rows, LANES), wide),
            pltpu.VMEM((requests, out_weight.shape[0]), low),
            pltpu.VMEM((requests, tile), wide),
            pltpu.VMEM((OUT_TILES, n, slots, tile), low),
            pltpu.VMEM((OUT_TILES, n, slots, tile), low),
            pltpu.SemaphoreType.DMA((3 + slots,)),
            pltpu.SemaphoreType.DMA((slots, n)),
            pltpu.SemaphoreType.DMA((slots, n)),
            pltpu.SemaphoreType.DMA((slots, n)),
            pltpu.SemaphoreType.DMA((slots, n)),
            pltpu.SemaphoreType.DMA((OUT_TILES, n)),
            pltpu.SemaphoreType.DMA((OUT_TILES, n)),
        ],
        compiler_params=pltpu.CompilerParams(
            collective_id=0, has_side_effects=True, vmem_limit_bytes=60 * 1024 * 1024
        ),
        name="decode",
    )(slot_request, lengths, queries, absorb_key, absorb_value, out_weight, cache)


def solution(mesh):
    return jax.shard_map(
        functools.partial(on_device, mesh.shape["req"]),
        mesh=mesh,
        in_specs=(
            P("groups", "req", None),
            P("req", None, None),
            P("req", None, None),
            P("req", None),
            P(("groups", "req"), None, None),
            P(("groups", "req")),
            P("groups"),
        ),
        out_specs=P(("groups", "req"), None),
        check_vma=False,
    )
```

```python
import functools
import math

import jax
import jax.numpy as jnp
from jax import lax
from jax.experimental import pallas as pl
from jax.experimental.pallas import tpu as pltpu
from jax.sharding import PartitionSpec as P

MESH = pl.DeviceIdType.MESH
LANES = 128
CORES = 2
SCORE_TILE = 1024
OUT_TILES = 5


def kernel(
    n, request_ref, length_ref, query_ref, key_hbm, value_hbm, weight_hbm, cache_hbm,
    out_ref,
    key, value, weight, cache, query_rows, rotary_rows, absorbed_rows, absorbed_out, absorbed_in,
    slot_rows, scores, latent_rows, latent_out, latent_in, returned_rows, values,
    partial, partner_rows, chip_rows, partial_out, partial_in,
    load_sem, send_a, recv_a, send_b, recv_b, send_p, recv_p, send_c, recv_c,
):
    requests, heads, width = query_ref.shape
    nope, latent = key_hbm.shape[1:]
    vdim = value_hbm.shape[2]
    slots, _, context = cache_hbm.shape
    tiles = partial_out.shape[0]
    tile = partial_out.shape[3]
    lanes = latent // LANES
    chips = n // CORES
    me = lax.axis_index("req")

    barrier = pltpu.get_barrier_semaphore()

    def greet(k, carry):
        pl.semaphore_signal(
            barrier, inc=1, device_id={"req": lax.rem(me + k, n)}, device_id_type=MESH
        )
        return carry

    lax.fori_loop(1, n, greet, 0)

    load_key = pltpu.make_async_copy(key_hbm, key, load_sem.at[0])
    load_value = pltpu.make_async_copy(value_hbm, value, load_sem.at[1])
    load_weight = pltpu.make_async_copy(weight_hbm, weight, load_sem.at[2])
    load_cache = [
        pltpu.make_async_copy(cache_hbm.at[s], cache.at[s], load_sem.at[3 + s])
        for s in range(slots)
    ]
    load_key.start()
    load_cache[0].start()

    for j in range(requests):
        row = query_ref[request_ref[j]].astype(jnp.float32)
        query_rows[j * heads : (j + 1) * heads, :] = row[:, :nope]
        rotary_rows[j * heads : (j + 1) * heads, :] = row[:, nope:]
    load_key.wait()
    for s in range(1, slots):
        load_cache[s].start()
    load_value.start()
    load_weight.start()
    for h in range(heads):
        picked = query_rows[pl.ds(h, requests, stride=heads), :].astype(jnp.bfloat16)
        lifted = jnp.dot(picked, key[h], preferred_element_type=jnp.float32)
        for l in range(lanes):
            absorbed_rows[l, pl.ds(h, requests, stride=heads), :] = lifted[
                :, l * LANES : (l + 1) * LANES
            ]

    def exchange(out, into, send_sem, recv_sem, at, stride=1):
        mine, count = lax.div(me, stride), n // stride

        def copy(to, source):
            return pltpu.make_async_remote_copy(
                src_ref=out.at[at, to],
                dst_ref=into.at[at, source],
                send_sem=send_sem.at[at, to],
                recv_sem=recv_sem.at[at, source],
                device_id={"req": to * stride + lax.rem(me, stride)},
                device_id_type=MESH,
            )

        def start(k, carry):
            copy(lax.rem(mine + k, count), mine).start()
            return carry

        def arrive(k, carry):
            other = lax.rem(mine + count - k, count)
            copy(other, other).wait_recv()
            return carry

        def leave(k, carry):
            copy(lax.rem(mine + k, count), mine).wait_send()
            return carry

        return (
            lambda: lax.fori_loop(1, count, start, 0),
            lambda: lax.fori_loop(1, count, arrive, 0),
            lambda: lax.fori_loop(1, count, leave, 0),
        )

    queries_of = [exchange(absorbed_out, absorbed_in, send_a, recv_a, s) for s in range(slots)]
    latents_of = [exchange(latent_out, latent_in, send_b, recv_b, s) for s in range(slots)]
    partials_of = [exchange(partial_out, partial_in, send_c, recv_c, c, CORES) for c in range(tiles)]

    for s in range(slots):
        for d in range(n):
            row = (d * slots + s) * heads
            for l in range(lanes):
                absorbed_out[s, d, :, l * LANES : (l + 1) * LANES] = absorbed_rows[
                    l, row : row + heads, :
                ].astype(jnp.bfloat16)
            absorbed_out[s, d, :, latent:] = rotary_rows[row : row + heads, :].astype(jnp.bfloat16)
        if s == 0:
            pl.semaphore_wait(barrier, n - 1)
        queries_of[s][0]()
        absorbed_in[s, me] = absorbed_out[s, me]

    scale = math.log2(math.e) / math.sqrt(width)
    for s in range(slots):
        queries_of[s][1]()
        for i in range(n):
            slot_rows[i * heads : (i + 1) * heads, :] = absorbed_in[s, i].astype(jnp.float32)
        query = slot_rows[...].astype(jnp.bfloat16)
        load_cache[s].wait()
        length = length_ref[s]
        highest = None
        for t in range(0, context, SCORE_TILE):
            score = jnp.dot(
                query, cache[s, :, t : t + SCORE_TILE], preferred_element_type=jnp.float32
            )
            position = t + lax.broadcasted_iota(jnp.int32, (1, SCORE_TILE), 1)
            score = jnp.where(position < length, score, -jnp.inf)
            scores[:, t : t + SCORE_TILE] = score
            top = jnp.max(score, axis=1, keepdims=True)
            highest = top if highest is None else jnp.maximum(highest, top)
        total, mixed = None, None
        for t in range(0, context, SCORE_TILE):
            prob = jnp.exp2((scores[:, t : t + SCORE_TILE] - highest) * scale)
            part = jnp.sum(prob, axis=1, keepdims=True)
            product = lax.dot_general(
                prob.astype(jnp.bfloat16),
                cache[s, :latent, t : t + SCORE_TILE],
                (((1,), (1,)), ((), ())),
                preferred_element_type=jnp.float32,
            )
            total = part if total is None else total + part
            mixed = product if mixed is None else mixed + product
        latent_rows[...] = mixed / total
        for i in range(n):
            latent_out[s, i] = latent_rows[i * heads : (i + 1) * heads, :].astype(jnp.bfloat16)
        latents_of[s][0]()
        latent_in[s, me] = latent_out[s, me]

    load_value.wait()
    for s in range(slots):
        latents_of[s][1]()
        for d in range(n):
            row = ((d % CORES * chips + d // CORES) * slots + s) * heads
            for l in range(lanes):
                returned_rows[l, row : row + heads, :] = latent_in[
                    s, d, :, l * LANES : (l + 1) * LANES
                ].astype(jnp.float32)
    for h in range(heads):
        picked = jnp.concatenate(
            [returned_rows[l, pl.ds(h, requests, stride=heads), :] for l in range(lanes)], axis=1
        ).astype(jnp.bfloat16)
        values[:, h * vdim : (h + 1) * vdim] = jnp.dot(
            picked, value[h], preferred_element_type=jnp.float32
        ).astype(jnp.bfloat16)

    load_weight.wait()
    core, chip = lax.rem(me, CORES), lax.div(me, CORES)
    pairs = [
        pltpu.make_async_remote_copy(
            src_ref=partial.at[c, CORES - 1 - core],
            dst_ref=partner_rows.at[c],
            send_sem=send_p.at[c],
            recv_sem=recv_p.at[c],
            device_id={"req": me + CORES - 1 - 2 * core},
            device_id_type=MESH,
        )
        for c in range(tiles)
    ]

    def pass_on(c):
        pairs[c].wait_recv()
        chip_rows[...] = partial[c, core] + partner_rows[c]
        for e in range(chips):
            partial_out[c, e] = chip_rows[e * slots : (e + 1) * slots, :].astype(jnp.bfloat16)
        partials_of[c][0]()
        partial_in[c, chip] = partial_out[c, chip]

    for c in range(tiles):
        product = jnp.dot(
            values[...], weight[:, c * tile : (c + 1) * tile], preferred_element_type=jnp.float32
        )
        for half in range(CORES):
            partial[c, half] = product[half * chips * slots : (half + 1) * chips * slots]
        pairs[c].start()
        if c > 0:
            pass_on(c - 1)
    pass_on(tiles - 1)
    for c in range(tiles):
        partials_of[c][1]()
        summed = partial_in[c, 0].astype(jnp.float32)
        for e in range(1, chips):
            summed = summed + partial_in[c, e].astype(jnp.float32)
        out_ref[:, c * tile : (c + 1) * tile] = summed.astype(jnp.bfloat16)
    for pair in pairs:
        pair.wait_send()

    for pending in queries_of + latents_of + partials_of:
        pending[2]()


def on_device(n, queries, absorb_key, absorb_value, out_weight, latent_cache, lengths, slot_request):
    cache = jnp.swapaxes(latent_cache, 1, 2)
    requests, heads, width = queries.shape
    slots, key_width, context = cache.shape
    nope, latent = absorb_key.shape[1:]
    model = out_weight.shape[1]
    rows = requests * heads
    tile, chips = model // OUT_TILES, n // CORES
    vmem, smem, anywhere = (
        pl.BlockSpec(memory_space=space) for space in (pltpu.VMEM, pltpu.SMEM, pl.ANY)
    )
    low, wide = jnp.bfloat16, jnp.float32
    return pl.pallas_call(
        functools.partial(kernel, n),
        out_shape=jax.ShapeDtypeStruct((slots, model), low),
        in_specs=[smem, smem, vmem, anywhere, anywhere, anywhere, anywhere],
        out_specs=vmem,
        scratch_shapes=[
            pltpu.VMEM(absorb_key.shape, low),
            pltpu.VMEM(absorb_value.shape, low),
            pltpu.VMEM(out_weight.shape, low),
            pltpu.VMEM(cache.shape, low),
            pltpu.VMEM((rows, nope), wide),
            pltpu.VMEM((rows, width - nope), wide),
            pltpu.VMEM((latent // LANES, rows, LANES), wide),
            pltpu.VMEM((slots, n, heads, key_width), low),
            pltpu.VMEM((slots, n, heads, key_width), low),
            pltpu.VMEM((n * heads, key_width), wide),
            pltpu.VMEM((n * heads, context), wide),
            pltpu.VMEM((n * heads, latent), wide),
            pltpu.VMEM((slots, n, heads, latent), low),
            pltpu.VMEM((slots, n, heads, latent), low),
            pltpu.VMEM((latent // LANES, rows, LANES), wide),
            pltpu.VMEM((requests, out_weight.shape[0]), low),
            pltpu.VMEM((OUT_TILES, CORES, chips * slots, tile), wide),
            pltpu.VMEM((OUT_TILES, chips * slots, tile), wide),
            pltpu.VMEM((chips * slots, tile), wide),
            pltpu.VMEM((OUT_TILES, chips, slots, tile), low),
            pltpu.VMEM((OUT_TILES, chips, slots, tile), low),
            pltpu.SemaphoreType.DMA((3 + slots,)),
            pltpu.SemaphoreType.DMA((slots, n)),
            pltpu.SemaphoreType.DMA((slots, n)),
            pltpu.SemaphoreType.DMA((slots, n)),
            pltpu.SemaphoreType.DMA((slots, n)),
            pltpu.SemaphoreType.DMA((OUT_TILES,)),
            pltpu.SemaphoreType.DMA((OUT_TILES,)),
            pltpu.SemaphoreType.DMA((OUT_TILES, chips)),
            pltpu.SemaphoreType.DMA((OUT_TILES, chips)),
        ],
        compiler_params=pltpu.CompilerParams(
            collective_id=0, has_side_effects=True, vmem_limit_bytes=60 * 1024 * 1024
        ),
        name="decode",
    )(slot_request, lengths, queries, absorb_key, absorb_value, out_weight, cache)


def solution(mesh):
    return jax.shard_map(
        functools.partial(on_device, mesh.shape["req"]),
        mesh=mesh,
        in_specs=(
            P("groups", "req", None),
            P("req", None, None),
            P("req", None, None),
            P("req", None),
            P(("groups", "req"), None, None),
            P(("groups", "req")),
            P("groups"),
        ),
        out_specs=P(("groups", "req"), None),
        check_vma=False,
    )
```

```python
import functools
import math

import jax
import jax.numpy as jnp
from jax import lax
from jax.experimental import pallas as pl
from jax.experimental.pallas import tpu as pltpu
from jax.sharding import PartitionSpec as P

MESH = pl.DeviceIdType.MESH
LANES = 128
CORES = 2
SCORE_TILE = 1024
OUT_TILES = 2


def kernel(
    n, request_hbm, length_hbm, query_hbm, key_hbm, value_hbm, weight_hbm, cache_hbm,
    out_ref,
    request_ref, length_ref, query_ref, key, value, weight, cache, query_rows, rotary_rows, absorbed_rows, absorbed_out, absorbed_in,
    slot_rows, scores, latent_rows, latent_out, latent_in, returned_rows, values,
    partial, partner_rows, chip_rows, partial_out, partial_in,
    small_sem, load_sem, send_a, recv_a, send_b, recv_b, send_p, recv_p, send_c, recv_c,
):
    requests, heads, width = query_ref.shape
    nope, latent = key_hbm.shape[1:]
    vdim = value_hbm.shape[2]
    slots, _, context = cache_hbm.shape
    tiles = partial_out.shape[0]
    tile = partial_out.shape[3]
    lanes = latent // LANES
    chips = n // CORES
    me = lax.axis_index("req")

    barrier = pltpu.get_barrier_semaphore()

    for k in range(1, n):
        pl.semaphore_signal(
            barrier, inc=1, device_id={"req": lax.rem(me + k, n)}, device_id_type=MESH
        )

    small = [
        pltpu.make_async_copy(source, into, small_sem.at[i])
        for i, (source, into) in enumerate(
            [(request_hbm, request_ref), (query_hbm, query_ref), (length_hbm, length_ref)]
        )
    ]
    for load in small:
        load.start()
    load_key = pltpu.make_async_copy(key_hbm, key, load_sem.at[0])
    load_value = pltpu.make_async_copy(value_hbm, value, load_sem.at[1])
    load_weight = pltpu.make_async_copy(weight_hbm, weight, load_sem.at[2])
    load_cache = [
        pltpu.make_async_copy(cache_hbm.at[s], cache.at[s], load_sem.at[3 + s])
        for s in range(slots)
    ]
    load_key.start()
    load_cache[0].start()

    for load in small:
        load.wait()
    for j in range(requests):
        row = query_ref[request_ref[j]].astype(jnp.float32)
        query_rows[j * heads : (j + 1) * heads, :] = row[:, :nope]
        rotary_rows[j * heads : (j + 1) * heads, :] = row[:, nope:]
    load_key.wait()
    for s in range(1, slots):
        load_cache[s].start()
    load_value.start()
    load_weight.start()
    for h in range(heads):
        picked = query_rows[pl.ds(h, requests, stride=heads), :].astype(jnp.bfloat16)
        lifted = jnp.dot(picked, key[h], preferred_element_type=jnp.float32)
        for l in range(lanes):
            absorbed_rows[l, pl.ds(h, requests, stride=heads), :] = lifted[
                :, l * LANES : (l + 1) * LANES
            ]

    def exchange(out, into, send_sem, recv_sem, at, stride=1):
        mine, count = lax.div(me, stride), n // stride

        def copy(to, source):
            return pltpu.make_async_remote_copy(
                src_ref=out.at[at, to],
                dst_ref=into.at[at, source],
                send_sem=send_sem.at[at],
                recv_sem=recv_sem.at[at],
                device_id={"req": to * stride + lax.rem(me, stride)},
                device_id_type=MESH,
            )

        def start():
            for k in range(1, count):
                copy(lax.rem(mine + k, count), mine).start()

        others = pl.ds(0, count - 1)

        def arrive():
            blocks = into.at[at, others]
            pltpu.make_async_copy(blocks, blocks, recv_sem.at[at]).wait()

        def leave():
            blocks = out.at[at, others]
            pltpu.make_async_copy(blocks, blocks, send_sem.at[at]).wait()

        return start, arrive, leave

    queries_of = [exchange(absorbed_out, absorbed_in, send_a, recv_a, s) for s in range(slots)]
    latents_of = [exchange(latent_out, latent_in, send_b, recv_b, s) for s in range(slots)]
    partials_of = [exchange(partial_out, partial_in, send_c, recv_c, c, CORES) for c in range(tiles)]

    for s in range(slots):
        for d in range(n):
            row = (d * slots + s) * heads
            for l in range(lanes):
                absorbed_out[s, d, :, l * LANES : (l + 1) * LANES] = absorbed_rows[
                    l, row : row + heads, :
                ].astype(jnp.bfloat16)
            absorbed_out[s, d, :, latent:] = rotary_rows[row : row + heads, :].astype(jnp.bfloat16)
        if s == 0:
            pl.semaphore_wait(barrier, n - 1)
        queries_of[s][0]()
        absorbed_in[s, me] = absorbed_out[s, me]

    scale = math.log2(math.e) / math.sqrt(width)
    for s in range(slots):
        queries_of[s][1]()
        for i in range(n):
            slot_rows[i * heads : (i + 1) * heads, :] = absorbed_in[s, i].astype(jnp.float32)
        query = slot_rows[...].astype(jnp.bfloat16)
        load_cache[s].wait()
        length = length_ref[s]
        highest = None
        for t in range(0, context, SCORE_TILE):
            score = jnp.dot(
                query, cache[s, :, t : t + SCORE_TILE], preferred_element_type=jnp.float32
            )
            position = t + lax.broadcasted_iota(jnp.int32, (1, SCORE_TILE), 1)
            score = jnp.where(position < length, score, -jnp.inf)
            scores[:, t : t + SCORE_TILE] = score
            top = jnp.max(score, axis=1, keepdims=True)
            highest = top if highest is None else jnp.maximum(highest, top)
        total, mixed = None, None
        for t in range(0, context, SCORE_TILE):
            prob = jnp.exp2((scores[:, t : t + SCORE_TILE] - highest) * scale)
            part = jnp.sum(prob, axis=1, keepdims=True)
            product = lax.dot_general(
                prob.astype(jnp.bfloat16),
                cache[s, :latent, t : t + SCORE_TILE],
                (((1,), (1,)), ((), ())),
                preferred_element_type=jnp.float32,
            )
            total = part if total is None else total + part
            mixed = product if mixed is None else mixed + product
        latent_rows[...] = mixed / total
        for i in range(n):
            latent_out[s, i] = latent_rows[i * heads : (i + 1) * heads, :].astype(jnp.bfloat16)
        latents_of[s][0]()
        latent_in[s, me] = latent_out[s, me]

    load_value.wait()
    for s in range(slots):
        latents_of[s][1]()
        for d in range(n):
            row = ((d % CORES * chips + d // CORES) * slots + s) * heads
            for l in range(lanes):
                returned_rows[l, row : row + heads, :] = latent_in[
                    s, d, :, l * LANES : (l + 1) * LANES
                ].astype(jnp.float32)
    for h in range(heads):
        picked = jnp.concatenate(
            [returned_rows[l, pl.ds(h, requests, stride=heads), :] for l in range(lanes)], axis=1
        ).astype(jnp.bfloat16)
        values[:, h * vdim : (h + 1) * vdim] = jnp.dot(
            picked, value[h], preferred_element_type=jnp.float32
        ).astype(jnp.bfloat16)

    load_weight.wait()
    core, chip = lax.rem(me, CORES), lax.div(me, CORES)
    pairs = [
        pltpu.make_async_remote_copy(
            src_ref=partial.at[c, CORES - 1 - core],
            dst_ref=partner_rows.at[c],
            send_sem=send_p.at[c],
            recv_sem=recv_p.at[c],
            device_id={"req": me + CORES - 1 - 2 * core},
            device_id_type=MESH,
        )
        for c in range(tiles)
    ]

    def pass_on(c):
        pairs[c].wait_recv()
        chip_rows[...] = partial[c, core] + partner_rows[c]
        for e in range(chips):
            partial_out[c, e] = chip_rows[e * slots : (e + 1) * slots, :].astype(jnp.bfloat16)
        partials_of[c][0]()
        partial_in[c, chip] = partial_out[c, chip]

    for c in range(tiles):
        product = jnp.dot(
            values[...], weight[:, c * tile : (c + 1) * tile], preferred_element_type=jnp.float32
        )
        for half in range(CORES):
            partial[c, half] = product[half * chips * slots : (half + 1) * chips * slots]
        pairs[c].start()
        if c > 0:
            pass_on(c - 1)
    pass_on(tiles - 1)
    for c in range(tiles):
        partials_of[c][1]()
        summed = partial_in[c, 0].astype(jnp.float32)
        for e in range(1, chips):
            summed = summed + partial_in[c, e].astype(jnp.float32)
        out_ref[:, c * tile : (c + 1) * tile] = summed.astype(jnp.bfloat16)
    for pair in pairs:
        pair.wait_send()

    for pending in queries_of + latents_of + partials_of:
        pending[2]()


def on_device(n, queries, absorb_key, absorb_value, out_weight, latent_cache, lengths, slot_request):
    cache = jnp.swapaxes(latent_cache, 1, 2)
    requests, heads, width = queries.shape
    slots, key_width, context = cache.shape
    nope, latent = absorb_key.shape[1:]
    model = out_weight.shape[1]
    rows = requests * heads
    tile, chips = model // OUT_TILES, n // CORES
    vmem, anywhere = (pl.BlockSpec(memory_space=space) for space in (pltpu.VMEM, pl.ANY))
    low, wide = jnp.bfloat16, jnp.float32
    return pl.pallas_call(
        functools.partial(kernel, n),
        out_shape=jax.ShapeDtypeStruct((slots, model), low),
        in_specs=[anywhere] * 7,
        out_specs=vmem,
        scratch_shapes=[
            pltpu.SMEM(slot_request.shape, jnp.int32),
            pltpu.SMEM(lengths.shape, jnp.int32),
            pltpu.VMEM(queries.shape, low),
            pltpu.VMEM(absorb_key.shape, low),
            pltpu.VMEM(absorb_value.shape, low),
            pltpu.VMEM(out_weight.shape, low),
            pltpu.VMEM(cache.shape, low),
            pltpu.VMEM((rows, nope), wide),
            pltpu.VMEM((rows, width - nope), wide),
            pltpu.VMEM((latent // LANES, rows, LANES), wide),
            pltpu.VMEM((slots, n, heads, key_width), low),
            pltpu.VMEM((slots, n, heads, key_width), low),
            pltpu.VMEM((n * heads, key_width), wide),
            pltpu.VMEM((n * heads, context), wide),
            pltpu.VMEM((n * heads, latent), wide),
            pltpu.VMEM((slots, n, heads, latent), low),
            pltpu.VMEM((slots, n, heads, latent), low),
            pltpu.VMEM((latent // LANES, rows, LANES), wide),
            pltpu.VMEM((requests, out_weight.shape[0]), low),
            pltpu.VMEM((OUT_TILES, CORES, chips * slots, tile), wide),
            pltpu.VMEM((OUT_TILES, chips * slots, tile), wide),
            pltpu.VMEM((chips * slots, tile), wide),
            pltpu.VMEM((OUT_TILES, chips, slots, tile), low),
            pltpu.VMEM((OUT_TILES, chips, slots, tile), low),
            pltpu.SemaphoreType.DMA((3,)),
            pltpu.SemaphoreType.DMA((3 + slots,)),
            pltpu.SemaphoreType.DMA((slots,)),
            pltpu.SemaphoreType.DMA((slots,)),
            pltpu.SemaphoreType.DMA((slots,)),
            pltpu.SemaphoreType.DMA((slots,)),
            pltpu.SemaphoreType.DMA((OUT_TILES,)),
            pltpu.SemaphoreType.DMA((OUT_TILES,)),
            pltpu.SemaphoreType.DMA((OUT_TILES,)),
            pltpu.SemaphoreType.DMA((OUT_TILES,)),
        ],
        compiler_params=pltpu.CompilerParams(
            collective_id=0, has_side_effects=True, vmem_limit_bytes=60 * 1024 * 1024
        ),
        name="decode",
    )(slot_request, lengths, queries, absorb_key, absorb_value, out_weight, cache)


def solution(mesh):
    return jax.shard_map(
        functools.partial(on_device, mesh.shape["req"]),
        mesh=mesh,
        in_specs=(
            P("groups", "req", None),
            P("req", None, None),
            P("req", None, None),
            P("req", None),
            P(("groups", "req"), None, None),
            P(("groups", "req")),
            P("groups"),
        ),
        out_specs=P(("groups", "req"), None),
        check_vma=False,
    )
```

```python
import functools
import math

import jax
import jax.numpy as jnp
from jax import lax
from jax.experimental import pallas as pl
from jax.experimental.pallas import tpu as pltpu
from jax.sharding import PartitionSpec as P

MESH = pl.DeviceIdType.MESH
LANES = 128
CORES = 2
SCORE_TILE = 1024


def kernel(
    n, request_hbm, length_hbm, query_hbm, key_hbm, value_hbm, weight_hbm, cache_hbm,
    out_ref,
    request_ref, length_ref, query_ref, key, value, weight, cache, query_rows, rotary_rows, absorbed_rows, absorbed_out, absorbed_in,
    slot_rows, scores, latent_rows, latent_out, latent_in, returned_rows, values,
    partial, partner_rows, chip_rows, partial_out, partial_in,
    small_sem, load_sem, send_a, recv_a, send_b, recv_b, send_p, recv_p, send_c, recv_c,
):
    requests, heads, width = query_ref.shape
    nope, latent = key_hbm.shape[1:]
    vdim = value_hbm.shape[2]
    slots, _, context = cache_hbm.shape
    lanes = latent // LANES
    chips = n // CORES
    me = lax.axis_index("req")

    barrier = pltpu.get_barrier_semaphore()

    for k in range(1, n):
        pl.semaphore_signal(
            barrier, inc=1, device_id={"req": lax.rem(me + k, n)}, device_id_type=MESH
        )

    small = [
        pltpu.make_async_copy(source, into, small_sem.at[i])
        for i, (source, into) in enumerate(
            [(request_hbm, request_ref), (query_hbm, query_ref), (length_hbm, length_ref)]
        )
    ]
    for load in small:
        load.start()
    load_key = pltpu.make_async_copy(key_hbm, key, load_sem.at[0])
    load_value = pltpu.make_async_copy(value_hbm, value, load_sem.at[1])
    load_weight = pltpu.make_async_copy(weight_hbm, weight, load_sem.at[2])
    load_cache = [
        pltpu.make_async_copy(cache_hbm.at[s], cache.at[s], load_sem.at[3 + s])
        for s in range(slots)
    ]
    load_key.start()
    load_cache[0].start()

    for load in small:
        load.wait()
    for j in range(requests):
        row = query_ref[request_ref[j]].astype(jnp.float32)
        query_rows[j * heads : (j + 1) * heads, :] = row[:, :nope]
        rotary_rows[j * heads : (j + 1) * heads, :] = row[:, nope:]
    load_key.wait()
    for s in range(1, slots):
        load_cache[s].start()
    load_value.start()
    load_weight.start()
    for h in range(heads):
        picked = query_rows[pl.ds(h, requests, stride=heads), :].astype(jnp.bfloat16)
        lifted = jnp.dot(picked, key[h], preferred_element_type=jnp.float32)
        for l in range(lanes):
            absorbed_rows[l, pl.ds(h, requests, stride=heads), :] = lifted[
                :, l * LANES : (l + 1) * LANES
            ]

    def exchange(out, into, send_sem, recv_sem, at, stride=1):
        mine, count = lax.div(me, stride), n // stride

        def copy(to, source):
            return pltpu.make_async_remote_copy(
                src_ref=out.at[at, to],
                dst_ref=into.at[at, source],
                send_sem=send_sem.at[at],
                recv_sem=recv_sem.at[at],
                device_id={"req": to * stride + lax.rem(me, stride)},
                device_id_type=MESH,
            )

        def start():
            for k in range(1, count):
                copy(lax.rem(mine + k, count), mine).start()

        others = pl.ds(0, count - 1)

        def arrive():
            blocks = into.at[at, others]
            pltpu.make_async_copy(blocks, blocks, recv_sem.at[at]).wait()

        def leave():
            blocks = out.at[at, others]
            pltpu.make_async_copy(blocks, blocks, send_sem.at[at]).wait()

        return start, arrive, leave

    queries_of = [exchange(absorbed_out, absorbed_in, send_a, recv_a, s) for s in range(slots)]
    latents_of = [exchange(latent_out, latent_in, send_b, recv_b, s) for s in range(slots)]
    partials_of = [exchange(partial_out, partial_in, send_c, recv_c, s, CORES) for s in range(slots)]

    for s in range(slots):
        for d in range(n):
            row = (d * slots + s) * heads
            for l in range(lanes):
                absorbed_out[s, d, :, l * LANES : (l + 1) * LANES] = absorbed_rows[
                    l, row : row + heads, :
                ].astype(jnp.bfloat16)
            absorbed_out[s, d, :, latent:] = rotary_rows[row : row + heads, :].astype(jnp.bfloat16)
        if s == 0:
            pl.semaphore_wait(barrier, n - 1)
        queries_of[s][0]()
        absorbed_in[s, me] = absorbed_out[s, me]

    scale = math.log2(math.e) / math.sqrt(width)
    for s in range(slots):
        queries_of[s][1]()
        for i in range(n):
            slot_rows[i * heads : (i + 1) * heads, :] = absorbed_in[s, i].astype(jnp.float32)
        query = slot_rows[...].astype(jnp.bfloat16)
        load_cache[s].wait()
        length = length_ref[s]
        highest = None
        for t in range(0, context, SCORE_TILE):
            score = jnp.dot(
                query, cache[s, :, t : t + SCORE_TILE], preferred_element_type=jnp.float32
            )
            position = t + lax.broadcasted_iota(jnp.int32, (1, SCORE_TILE), 1)
            score = jnp.where(position < length, score, -jnp.inf)
            scores[:, t : t + SCORE_TILE] = score
            top = jnp.max(score, axis=1, keepdims=True)
            highest = top if highest is None else jnp.maximum(highest, top)
        total, mixed = None, None
        for t in range(0, context, SCORE_TILE):
            prob = jnp.exp2((scores[:, t : t + SCORE_TILE] - highest) * scale)
            part = jnp.sum(prob, axis=1, keepdims=True)
            product = lax.dot_general(
                prob.astype(jnp.bfloat16),
                cache[s, :latent, t : t + SCORE_TILE],
                (((1,), (1,)), ((), ())),
                preferred_element_type=jnp.float32,
            )
            total = part if total is None else total + part
            mixed = product if mixed is None else mixed + product
        latent_rows[...] = mixed / total
        for i in range(n):
            latent_out[s, i] = latent_rows[i * heads : (i + 1) * heads, :].astype(jnp.bfloat16)
        latents_of[s][0]()
        latent_in[s, me] = latent_out[s, me]

    core, chip = lax.rem(me, CORES), lax.div(me, CORES)
    pairs = [
        pltpu.make_async_remote_copy(
            src_ref=partial.at[s, CORES - 1 - core],
            dst_ref=partner_rows.at[s],
            send_sem=send_p.at[s],
            recv_sem=recv_p.at[s],
            device_id={"req": me + CORES - 1 - 2 * core},
            device_id_type=MESH,
        )
        for s in range(slots)
    ]
    half = out_ref.shape[1] // 2
    load_value.wait()
    load_weight.wait()
    for s in range(slots):
        latents_of[s][1]()
        for d in range(n):
            row = ((s * CORES + d % CORES) * chips + d // CORES) * heads
            for l in range(lanes):
                returned_rows[l, row : row + heads, :] = latent_in[
                    s, d, :, l * LANES : (l + 1) * LANES
                ].astype(jnp.float32)
        for h in range(heads):
            rows = pl.ds(s * n * heads + h, n, stride=heads)
            picked = jnp.concatenate(
                [returned_rows[l, rows, :] for l in range(lanes)], axis=1
            ).astype(jnp.bfloat16)
            values[s, :, h * vdim : (h + 1) * vdim] = jnp.dot(
                picked, value[h], preferred_element_type=jnp.float32
            ).astype(jnp.bfloat16)
        product = jnp.dot(values[s], weight[...], preferred_element_type=jnp.float32)
        for c in range(CORES):
            partial[s, c] = product[c * chips : (c + 1) * chips]
        pairs[s].start()
        pairs[s].wait_recv()
        chip_rows[...] = partial[s, core] + partner_rows[s]
        for e in range(chips):
            partial_out[s, e] = jnp.concatenate(
                [chip_rows[e : e + 1, :half], chip_rows[e : e + 1, half:]], axis=0
            ).astype(jnp.bfloat16)
        partials_of[s][0]()
        partial_in[s, chip] = partial_out[s, chip]
    sums = []
    for s in range(slots):
        partials_of[s][1]()
        summed = partial_in[s, 0].astype(jnp.float32)
        for e in range(1, chips):
            summed = summed + partial_in[s, e].astype(jnp.float32)
        sums.append(summed)
    for c in range(2):
        out_ref[:, c * half : (c + 1) * half] = jnp.concatenate(
            [summed[c : c + 1] for summed in sums], axis=0
        ).astype(jnp.bfloat16)
    for pair in pairs:
        pair.wait_send()

    for pending in queries_of + latents_of + partials_of:
        pending[2]()


def on_device(n, queries, absorb_key, absorb_value, out_weight, latent_cache, lengths, slot_request):
    cache = jnp.swapaxes(latent_cache, 1, 2)
    requests, heads, width = queries.shape
    slots, key_width, context = cache.shape
    nope, latent = absorb_key.shape[1:]
    model = out_weight.shape[1]
    rows = requests * heads
    chips = n // CORES
    vmem, anywhere = (pl.BlockSpec(memory_space=space) for space in (pltpu.VMEM, pl.ANY))
    low, wide = jnp.bfloat16, jnp.float32
    return pl.pallas_call(
        functools.partial(kernel, n),
        out_shape=jax.ShapeDtypeStruct((slots, model), low),
        in_specs=[anywhere] * 7,
        out_specs=vmem,
        scratch_shapes=[
            pltpu.SMEM(slot_request.shape, jnp.int32),
            pltpu.SMEM(lengths.shape, jnp.int32),
            pltpu.VMEM(queries.shape, low),
            pltpu.VMEM(absorb_key.shape, low),
            pltpu.VMEM(absorb_value.shape, low),
            pltpu.VMEM(out_weight.shape, low),
            pltpu.VMEM(cache.shape, low),
            pltpu.VMEM((rows, nope), wide),
            pltpu.VMEM((rows, width - nope), wide),
            pltpu.VMEM((latent // LANES, rows, LANES), wide),
            pltpu.VMEM((slots, n, heads, key_width), low),
            pltpu.VMEM((slots, n, heads, key_width), low),
            pltpu.VMEM((n * heads, key_width), wide),
            pltpu.VMEM((n * heads, context), wide),
            pltpu.VMEM((n * heads, latent), wide),
            pltpu.VMEM((slots, n, heads, latent), low),
            pltpu.VMEM((slots, n, heads, latent), low),
            pltpu.VMEM((latent // LANES, rows, LANES), wide),
            pltpu.VMEM((slots, n, out_weight.shape[0]), low),
            pltpu.VMEM((slots, CORES, chips, model), wide),
            pltpu.VMEM((slots, chips, model), wide),
            pltpu.VMEM((chips, model), wide),
            pltpu.VMEM((slots, chips, 2, model // 2), low),
            pltpu.VMEM((slots, chips, 2, model // 2), low),
            pltpu.SemaphoreType.DMA((3,)),
            pltpu.SemaphoreType.DMA((3 + slots,)),
            pltpu.SemaphoreType.DMA((slots,)),
            pltpu.SemaphoreType.DMA((slots,)),
            pltpu.SemaphoreType.DMA((slots,)),
            pltpu.SemaphoreType.DMA((slots,)),
            pltpu.SemaphoreType.DMA((slots,)),
            pltpu.SemaphoreType.DMA((slots,)),
            pltpu.SemaphoreType.DMA((slots,)),
            pltpu.SemaphoreType.DMA((slots,)),
        ],
        compiler_params=pltpu.CompilerParams(
            collective_id=0, has_side_effects=True, vmem_limit_bytes=60 * 1024 * 1024
        ),
        name="decode",
    )(slot_request, lengths, queries, absorb_key, absorb_value, out_weight, cache)


def solution(mesh):
    return jax.shard_map(
        functools.partial(on_device, mesh.shape["req"]),
        mesh=mesh,
        in_specs=(
            P("groups", "req", None),
            P("req", None, None),
            P("req", None, None),
            P("req", None),
            P(("groups", "req"), None, None),
            P(("groups", "req")),
            P("groups"),
        ),
        out_specs=P(("groups", "req"), None),
        check_vma=False,
    )
```
